32 devices in a mesh: gx: 8 (over z, core), gy: 4 (over y, x).
Axes of the slice: x: 2, y: 2, z: 4, core: 2. Of those that a mesh axis runs over, the one named last changes fastest.
Arguments:
- right_side: float32 [8, 256, 1024], P(None, 'gx', 'gy'), may hold values from -6 to 6
- conductivity: float32 [8, 256, 1024], P(None, 'gx', 'gy'), may hold values from 0.1 to 1
Outputs:
- solution_field: float32 [8, 256, 1024], P(None, 'gx', 'gy')
- residual: float32 [8, 256, 1024], P(None, 'gx', 'gy')
The draws below stay inside these ranges and needn't reach their ends.
All inputs are finite; a program needn't handle non-finite values.
Results may differ from the reference program's by a relative error of at most 0.0003.
Values sent between devices are 32-bit elements; how exact they have to be, the bound alone decides.
A program may use at most 64 MiB of HBM per device.

```python
import math
import jax
import jax.numpy as jnp

LZ = 8
ITERS = 2
NX = 256
NY = 1024


def block_levels(stream_key, dims, shards, low, high):
    factor_of, own = 1.0, jax.random.fold_in(stream_key, 6)
    for position, blocks in shards:
        heights = jnp.exp(jax.random.uniform(jax.random.fold_in(own, position), (blocks,), jnp.float32, low / len(shards), high / len(shards)))
        factor_of = factor_of * jnp.repeat(heights, dims[position] // blocks).reshape([-1 if axis == position else 1 for axis in range(len(dims))])
    return factor_of


def gaussian(rng, shape, width, reach, pieces=(), held_as=jnp.bfloat16):
    entries = width * jax.random.normal(rng, shape, jnp.float32)
    if pieces:
        entries = entries * block_levels(rng, shape, pieces, -0.22, 0.18)
    return jnp.clip(entries, -reach, reach).astype(held_as)


def setup_inputs(seed: int = 0) -> dict:
    key_of = jax.random.split(jax.random.key(seed), 3)
    return {
        "right_side": gaussian(key_of[0], (LZ, NX, NY), 1.0, 6.0, ((1, 8), (2, 4)), jnp.float32),
        "conductivity": jnp.clip(jnp.exp(math.log(1.0) - 2.3025851 * jax.random.uniform(key_of[1], (LZ, NX, NY), jnp.float32) ** block_levels(key_of[1], (LZ, NX, NY), ((1, 8), (2, 4)), -0.2, 0.2)), 0.1, 1.0),
    }


low_bound = 0.4
high_bound = 12.0
cheb_theta = 0.5 * (high_bound + low_bound)
cheb_delta = 0.5 * (high_bound - low_bound)
cheb_sigma = cheb_theta / cheb_delta
rho_first = 1.0 / cheb_sigma
rho_second = 1.0 / (2.0 * cheb_sigma - rho_first)
rho_third = 1.0 / (2.0 * cheb_sigma - rho_second)
neighbours = ((1, 0, 0), (-1, 0, 0), (0, 1, 0), (0, -1, 0), (0, 0, 1), (0, 0, -1))


def shifted(padded, dz, dx, dy):
    return padded[1 + dz:padded.shape[0] - 1 + dz, 1 + dx:padded.shape[1] - 1 + dx, 1 + dy:padded.shape[2] - 1 + dy]


def stencil(field_pad, cond_pad):
    field_full = jnp.pad(field_pad, ((1, 1), (0, 0), (0, 0)))
    cond_full = jnp.pad(cond_pad, ((1, 1), (0, 0), (0, 0)))
    centre = shifted(field_full, 0, 0, 0)
    cond_centre = shifted(cond_full, 0, 0, 0)
    total = jnp.zeros_like(centre)
    for dz, dx, dy in neighbours:
        total = total + 0.5 * (cond_centre + shifted(cond_full, dz, dx, dy)) * (centre - shifted(field_full, dz, dx, dy))
    return total


def reference(right_side, conductivity):
    cond_pad = jnp.pad(conductivity, ((0, 0), (1, 1), (1, 1)))

    def operate(field):
        return stencil(jnp.pad(field, ((0, 0), (1, 1), (1, 1))), cond_pad)

    def chain(source):
        first = source / cheb_theta
        res_one = source - operate(first)
        step_one = rho_second * rho_first * first + (2.0 * rho_second / cheb_delta) * res_one
        second = first + step_one
        res_two = res_one - operate(step_one)
        step_two = rho_third * rho_second * step_one + (2.0 * rho_third / cheb_delta) * res_two
        precond = second + step_two
        return precond, operate(precond)

    solution_field = jnp.zeros_like(right_side)
    residual = right_side
    precond, applied = chain(residual)
    gamma_old = jnp.float32(1.0)
    alpha_old = jnp.float32(1.0)
    direction = dir_image = dir_precond = dir_double = None
    for iteration in range(ITERS):
        gamma_now = jnp.sum(residual * precond)
        delta_now = jnp.sum(applied * precond)
        pre_applied, image = chain(applied)
        if iteration == 0:
            alpha_now = gamma_now / delta_now
            dir_double, dir_precond, dir_image, direction = image, pre_applied, applied, precond
        else:
            beta_now = gamma_now / gamma_old
            alpha_now = gamma_now / (delta_now - beta_now * gamma_now / alpha_old)
            dir_double = image + beta_now * dir_double
            dir_precond = pre_applied + beta_now * dir_precond
            dir_image = applied + beta_now * dir_image
            direction = precond + beta_now * direction
        solution_field = solution_field + alpha_now * direction
        residual = residual - alpha_now * dir_image
        precond = precond - alpha_now * dir_precond
        applied = applied - alpha_now * dir_double
        gamma_old = gamma_now
        alpha_old = alpha_now
    return solution_field, residual
```

```python
import jax
import jax.numpy as jnp
from jax import lax
from jax.experimental import pallas as pl
from jax.experimental.pallas import tpu as pltpu
from jax.sharding import PartitionSpec as P

low_bound = 0.4
high_bound = 12.0
cheb_theta = 0.5 * (high_bound + low_bound)
cheb_delta = 0.5 * (high_bound - low_bound)
cheb_sigma = cheb_theta / cheb_delta
rho_first = 1.0 / cheb_sigma
rho_second = 1.0 / (2.0 * cheb_sigma - rho_first)
rho_third = 1.0 / (2.0 * cheb_sigma - rho_second)

HALO = 6
LANES = 128
STRIP = 8
GROUP = 8
STEP = 2
MESH = pl.DeviceIdType.MESH
WAYS = ((-1, 0), (1, 0), (0, -1), (0, 1), (-1, -1), (-1, 1), (1, -1), (1, 1))


def kernel(
    num_x, num_y, r_hbm, c_hbm, x_out, res_out,
    r_in, c_in, rc, coef, step_f, res_f, prec, appl, pre2, img,
    packed, side_in, corner_in, turned, msg, from_x, from_y,
    in_sem, halo_send, halo_recv, x_send, x_recv, y_send, y_recv,
):
    levels, rows, cols = r_in.shape
    wide = cols + LANES
    tiles = rows // GROUP
    me_x = lax.axis_index("gx")
    me_y = lax.axis_index("gy")

    def exists(dx, dy):
        ok = jnp.bool_(True)
        if dx < 0:
            ok = me_x > 0
        if dx > 0:
            ok = me_x < num_x - 1
        if dy < 0:
            ok_y = me_y > 0
            ok = ok_y if dx == 0 else jnp.logical_and(ok, ok_y)
        if dy > 0:
            ok_y = me_y < num_y - 1
            ok = ok_y if dx == 0 else jnp.logical_and(ok, ok_y)
        return ok

    loads = [
        pltpu.make_async_copy(r_hbm, r_in, in_sem.at[0]),
        pltpu.make_async_copy(c_hbm, c_in, in_sem.at[1]),
    ]
    for load in loads:
        load.start()

    barrier = pltpu.get_barrier_semaphore()
    expected = jnp.int32(num_x - 1 + num_y - 1)
    for dx, dy in WAYS[4:]:
        ok = exists(dx, dy)

        @pl.when(ok)
        def _():
            pl.semaphore_signal(
                barrier, inc=1, device_id=(me_x + dx, me_y + dy), device_id_type=MESH
            )

        expected = expected + ok.astype(jnp.int32)
    for k in range(1, num_x):
        pl.semaphore_signal(
            barrier, inc=1, device_id=(lax.rem(me_x + k, num_x), me_y), device_id_type=MESH
        )
    for k in range(1, num_y):
        pl.semaphore_signal(
            barrier, inc=1, device_id=(me_x, lax.rem(me_y + k, num_y)), device_id_type=MESH
        )

    lane = lax.broadcasted_iota(jnp.int32, (levels, LANES), 1)

    for load in loads:
        load.wait()
    for a, source in enumerate((r_in, c_in)):
        for t in range(tiles):
            rc[a, HALO + t * GROUP : HALO + (t + 1) * GROUP, :, 0:cols] = jnp.transpose(
                source[:, t * GROUP : (t + 1) * GROUP, :], (1, 0, 2)
            )
    for side in range(2):
        first_lane = 0 if side == 0 else cols - LANES
        offset = 0 if side == 0 else LANES - STRIP
        for t in range(tiles):
            acc = jnp.zeros((levels, LANES), jnp.float32)
            for a in range(2):
                for g in range(GROUP):
                    place = (a * GROUP + g) * STRIP
                    moved = pltpu.roll(
                        rc[a, HALO + t * GROUP + g, :, first_lane : first_lane + LANES],
                        (place - offset) % LANES,
                        1,
                    )
                    acc = jnp.where((lane >= place) & (lane < place + STRIP), moved, acc)
            packed[side, t] = acc

    pl.semaphore_wait(barrier, expected)

    def halo_copy(way):
        dx, dy = WAYS[way]
        if dy == 0:
            src = rc.at[:, pl.ds(HALO if dx < 0 else rows, HALO), :, pl.ds(0, cols)]
            dst = rc.at[:, pl.ds(HALO + rows if dx < 0 else 0, HALO), :, pl.ds(0, cols)]
        elif dx == 0:
            src = packed.at[0 if dy < 0 else 1]
            dst = side_in.at[0 if dy < 0 else 1]
        else:
            src = packed.at[0 if dy < 0 else 1, 0 if dx < 0 else tiles - 1]
            dst = corner_in.at[way - 4]
        return pltpu.make_async_remote_copy(
            src_ref=src, dst_ref=dst, send_sem=halo_send.at[way], recv_sem=halo_recv.at[way],
            device_id=(me_x + dx, me_y + dy), device_id_type=MESH,
        )

    order = (4, 5, 6, 7, 0, 1, 2, 3)
    for way in order:

        @pl.when(exists(*WAYS[way]))
        def _():
            halo_copy(way).start()

    for way in order:
        dx, dy = WAYS[way]
        absent = jnp.logical_not(exists(-dx, -dy))

        @pl.when(absent)
        def _():
            if dy == 0:
                low = HALO + rows if dx < 0 else 0
                rc[:, low : low + HALO, :, 0:cols] = jnp.zeros(
                    (2, HALO, levels, cols), jnp.float32
                )
            elif dx == 0:
                side_in[0 if dy < 0 else 1] = jnp.zeros((tiles, levels, LANES), jnp.float32)
            else:
                corner_in[way - 4] = jnp.zeros((levels, LANES), jnp.float32)

    for way in order:
        dx, dy = WAYS[way]

        @pl.when(exists(-dx, -dy))
        def _():
            halo_copy(way).wait_recv()

    for row in range(rows + 2 * HALO):
        if row < HALO:
            right, left, g = corner_in[2], corner_in[3], row + GROUP - HALO
        elif row < HALO + rows:
            t, g = divmod(row - HALO, GROUP)
            right, left = side_in[0, t], side_in[1, t]
        else:
            right, left, g = corner_in[0], corner_in[1], row - HALO - rows
        for a in range(2):
            place = (a * GROUP + g) * STRIP
            right_moved = pltpu.roll(right, (LANES - place) % LANES, 1)
            left_moved = pltpu.roll(left, (2 * LANES - STRIP - place) % LANES, 1)
            rc[a, row, :, cols:wide] = jnp.where(
                lane < STRIP, right_moved, jnp.where(lane >= LANES - STRIP, left_moved, 0.0)
            )

    field = rc.at[0]
    cond = rc.at[1]
    level = lax.broadcasted_iota(jnp.int32, (STEP, levels, wide), 1)

    def around(v):
        return (
            pltpu.roll(v, 1, 2),
            pltpu.roll(v, wide - 1, 2),
            pltpu.roll(v, 1, 1),
            pltpu.roll(v, levels - 1, 1),
        )

    def coefficients(x):
        c = cond[pl.ds(x, STEP)]
        west, east, below, above = around(c)
        below = jnp.where(level > 0, below, 0.0)
        above = jnp.where(level < levels - 1, above, 0.0)
        inside = c > 0.0
        faces = [
            jnp.where(inside, 0.5 * (c + other), 0.0)
            for other in (cond[pl.ds(x - 1, STEP)], cond[pl.ds(x + 1, STEP)], west, east, below, above)
        ]
        diag = ((faces[0] + faces[1]) + (faces[2] + faces[3])) + (faces[4] + faces[5])
        faces[4] = jnp.where(level > 0, faces[4], 0.0)
        faces[5] = jnp.where(level < levels - 1, faces[5], 0.0)
        return [diag] + faces

    def apply(ref, x, k):
        v = ref[pl.ds(x, STEP)]
        west, east, below, above = around(v)
        off = (
            (k[1] * ref[pl.ds(x - 1, STEP)] + k[2] * ref[pl.ds(x + 1, STEP)])
            + (k[3] * west + k[4] * east)
        ) + (k[5] * below + k[6] * above)
        return v, k[0] * v - off

    def kept(x):
        return [coef[i, pl.ds(x, STEP)] for i in range(7)]

    def sweep(low, body, carry=None):
        def at(i, state):
            return body(low + i * STEP, state)

        return lax.fori_loop(0, (rows + 2 * HALO - 2 * low) // STEP, at, carry)

    def opening(ref, x, k):
        v, image = apply(ref, x, k)
        res_one = v - image * (1.0 / cheb_theta)
        res_f[pl.ds(x, STEP)] = res_one
        step_f[pl.ds(x, STEP)] = (
            (rho_second * rho_first / cheb_theta) * v + (2.0 * rho_second / cheb_delta) * res_one
        )

    def closing(source, out, x):
        step_one, image = apply(step_f, x, kept(x))
        res_two = res_f[pl.ds(x, STEP)] - image
        out[pl.ds(x, STEP)] = (
            (1.0 / cheb_theta) * source[pl.ds(x, STEP)]
            + (1.0 + rho_third * rho_second) * step_one
            + (2.0 * rho_third / cheb_delta) * res_two
        )

    def sweep_one(x, state):
        k = coefficients(x)
        for i in range(7):
            coef[i, pl.ds(x, STEP)] = k[i]
        opening(field, x, k)
        return state

    def sweep_two(x, state):
        closing(field, prec, x)
        return state

    def sweep_three(x, state):
        appl[pl.ds(x, STEP)] = apply(prec, x, kept(x))[1]
        return state

    def sweep_four(x, state):
        opening(appl, x, kept(x))
        return state

    def sweep_five(x, state):
        closing(appl, pre2, x)
        return state

    def folded(v):
        total = v[0]
        for i in range(1, STEP):
            total = total + v[i]
        parts = [total[:, i : i + LANES] for i in range(0, cols, LANES)]
        out = parts[0]
        for part in parts[1:]:
            out = out + part
        return out

    def sweep_six(x, state):
        m_all, n_all = apply(pre2, x, kept(x))
        img[pl.ds(x, STEP)] = n_all[:, :, 0:cols]
        m, n = m_all[:, :, 0:cols], n_all[:, :, 0:cols]
        r = field[pl.ds(x, STEP), :, 0:cols]
        p = prec[pl.ds(x, STEP), :, 0:cols]
        w = appl[pl.ds(x, STEP), :, 0:cols]
        products = (r * p, w * p, r * m, w * m, n * p, n * m)
        return tuple(s + folded(v) for s, v in zip(state, products))

    sweep(1, sweep_one)
    sweep(2, sweep_two)
    sweep(3, sweep_three)
    sweep(4, sweep_four)
    sweep(5, sweep_five)
    zero = jnp.zeros((levels, LANES), jnp.float32)
    sums = sweep(6, sweep_six, (zero,) * 6)

    line = lax.broadcasted_iota(jnp.int32, (8, LANES), 0)
    table = jnp.zeros((8, LANES), jnp.float32)
    for i, s in enumerate(sums):
        table = jnp.where(line == i, jnp.sum(s, axis=0, keepdims=True), table)
    msg[0] = table

    def turn(slot, ref):
        for t in range(tiles):
            turned[slot, :, t * GROUP : (t + 1) * GROUP, :] = jnp.transpose(
                ref[HALO + t * GROUP : HALO + (t + 1) * GROUP, :, 0:cols], (1, 0, 2)
            )

    copies = []
    for k in range(1, num_x):
        copies.append(pltpu.make_async_remote_copy(
            src_ref=msg.at[0], dst_ref=from_x.at[k - 1],
            send_sem=x_send.at[k - 1], recv_sem=x_recv.at[k - 1],
            device_id=(lax.rem(me_x + k, num_x), me_y), device_id_type=MESH,
        ))
    for copy in copies:
        copy.start()
    turn(0, prec)
    turn(1, appl)
    for copy in copies:
        copy.wait_recv()
    total = msg[0]
    for k in range(1, num_x):
        total = total + from_x[k - 1]
    msg[1] = total
    more = []
    for k in range(1, num_y):
        more.append(pltpu.make_async_remote_copy(
            src_ref=msg.at[1], dst_ref=from_y.at[k - 1],
            send_sem=y_send.at[k - 1], recv_sem=y_recv.at[k - 1],
            device_id=(me_x, lax.rem(me_y + k, num_y)), device_id_type=MESH,
        ))
    for copy in more:
        copy.start()
    turn(2, pre2)
    turn(3, img)
    for copy in more:
        copy.wait_recv()
    total = msg[1]
    for k in range(1, num_y):
        total = total + from_y[k - 1]

    def lanes_of(i):
        return total[i : i + 1, :]

    rp, wp, rm, wm, np_, nm = (lanes_of(i) for i in range(6))
    gamma_old = jnp.sum(rp, axis=1, keepdims=True)
    alpha_old = gamma_old / jnp.sum(wp, axis=1, keepdims=True)
    gamma = jnp.sum((rp - alpha_old * wp) - alpha_old * (rm - alpha_old * wm), axis=1, keepdims=True)
    delta = jnp.sum((wp - alpha_old * np_) - alpha_old * (wm - alpha_old * nm), axis=1, keepdims=True)
    beta = gamma / gamma_old
    alpha = gamma / (delta - beta * gamma / alpha_old)
    near = alpha_old + alpha * (1.0 + beta)
    far = alpha * alpha_old
    for z in range(levels):
        x_out[z] = near * turned[0, z] - far * turned[2, z]
        res_out[z] = (r_in[z] - near * turned[1, z]) + far * turned[3, z]

    for way in order:

        @pl.when(exists(*WAYS[way]))
        def _():
            halo_copy(way).wait_send()

    for copy in copies + more:
        copy.wait_send()


def solution(mesh):
    num_x, num_y = mesh.shape["gx"], mesh.shape["gy"]

    def per_device(right_side, conductivity):
        levels, rows, cols = right_side.shape
        high = rows + 2 * HALO
        wide = cols + LANES
        tiles = rows // GROUP

        def body(*refs):
            kernel(num_x, num_y, *refs)

        block = (levels, rows, cols)
        full = (high, levels, wide)
        out = jax.ShapeDtypeStruct(block, jnp.float32)
        vmem = lambda shape: pltpu.VMEM(shape, jnp.float32)
        dma = lambda n: pltpu.SemaphoreType.DMA((n,))
        return pl.pallas_call(
            body,
            out_shape=(out, out),
            in_specs=[pl.BlockSpec(memory_space=pl.ANY)] * 2,
            out_specs=(pl.BlockSpec(memory_space=pltpu.VMEM),) * 2,
            scratch_shapes=[
                vmem(block), vmem(block), vmem((2,) + full), vmem((7,) + full),
                vmem(full), vmem(full), vmem(full), vmem(full), vmem(full),
                vmem((high, levels, cols)),
                vmem((2, tiles, levels, LANES)), vmem((2, tiles, levels, LANES)),
                vmem((4, levels, LANES)), vmem((4,) + block),
                vmem((2, 8, LANES)), vmem((max(num_x - 1, 1), 8, LANES)),
                vmem((max(num_y - 1, 1), 8, LANES)),
                dma(2), dma(8), dma(8),
                dma(max(num_x - 1, 1)), dma(max(num_x - 1, 1)),
                dma(max(num_y - 1, 1)), dma(max(num_y - 1, 1)),
            ],
            compiler_params=pltpu.CompilerParams(
                collective_id=0, has_side_effects=True, vmem_limit_bytes=32 * 1024 * 1024
            ),
        )(right_side, conductivity)

    return jax.shard_map(
        per_device,
        mesh=mesh,
        in_specs=(P(None, "gx", "gy"), P(None, "gx", "gy")),
        out_specs=(P(None, "gx", "gy"), P(None, "gx", "gy")),
        check_vma=False,
    )
```

```python
import jax
import jax.numpy as jnp
from jax import lax
from jax.experimental import pallas as pl
from jax.experimental.pallas import tpu as pltpu
from jax.sharding import PartitionSpec as P

low_bound = 0.4
high_bound = 12.0
cheb_theta = 0.5 * (high_bound + low_bound)
cheb_delta = 0.5 * (high_bound - low_bound)
cheb_sigma = cheb_theta / cheb_delta
rho_first = 1.0 / cheb_sigma
rho_second = 1.0 / (2.0 * cheb_sigma - rho_first)
rho_third = 1.0 / (2.0 * cheb_sigma - rho_second)

HALO = 6
LANES = 128
STRIP = 8
GROUP = 8
STEP = 2
MESH = pl.DeviceIdType.MESH
WAYS = ((-1, 0), (1, 0), (0, -1), (0, 1), (-1, -1), (-1, 1), (1, -1), (1, 1))


def kernel(
    num_x, num_y, r_hbm, c_hbm, x_out, res_out,
    r_in, c_in, rc, coef, step_f, res_f, prec, appl, pre2, img,
    packed, side_in, corner_in, turned, msg, from_x, from_y,
    in_sem, halo_send, halo_recv, x_send, x_recv, y_send, y_recv,
):
    levels, rows, cols = r_in.shape
    wide = cols + LANES
    tiles = rows // GROUP
    me_x = lax.axis_index("gx")
    me_y = lax.axis_index("gy")

    def exists(dx, dy):
        ok = jnp.bool_(True)
        if dx < 0:
            ok = me_x > 0
        if dx > 0:
            ok = me_x < num_x - 1
        if dy < 0:
            ok_y = me_y > 0
            ok = ok_y if dx == 0 else jnp.logical_and(ok, ok_y)
        if dy > 0:
            ok_y = me_y < num_y - 1
            ok = ok_y if dx == 0 else jnp.logical_and(ok, ok_y)
        return ok

    loads = [
        pltpu.make_async_copy(r_hbm, r_in, in_sem.at[0]),
        pltpu.make_async_copy(c_hbm, c_in, in_sem.at[1]),
    ]
    for load in loads:
        load.start()

    barrier = pltpu.get_barrier_semaphore()
    expected = jnp.int32(num_x - 1 + num_y - 1)
    for dx, dy in WAYS[4:]:
        ok = exists(dx, dy)

        @pl.when(ok)
        def _():
            pl.semaphore_signal(
                barrier, inc=1, device_id=(me_x + dx, me_y + dy), device_id_type=MESH
            )

        expected = expected + ok.astype(jnp.int32)
    for k in range(1, num_x):
        pl.semaphore_signal(
            barrier, inc=1, device_id=(lax.rem(me_x + k, num_x), me_y), device_id_type=MESH
        )
    for k in range(1, num_y):
        pl.semaphore_signal(
            barrier, inc=1, device_id=(me_x, lax.rem(me_y + k, num_y)), device_id_type=MESH
        )

    lane = lax.broadcasted_iota(jnp.int32, (levels, LANES), 1)

    for load in loads:
        load.wait()
    for a, source in enumerate((r_in, c_in)):
        for t in range(tiles):
            rc[a, HALO + t * GROUP : HALO + (t + 1) * GROUP, :, 0:cols] = jnp.transpose(
                source[:, t * GROUP : (t + 1) * GROUP, :], (1, 0, 2)
            )
    for side in range(2):
        first_lane = 0 if side == 0 else cols - LANES
        offset = 0 if side == 0 else LANES - STRIP
        for t in range(tiles):
            acc = jnp.zeros((levels, LANES), jnp.float32)
            for a in range(2):
                for g in range(GROUP):
                    place = (a * GROUP + g) * STRIP
                    moved = pltpu.roll(
                        rc[a, HALO + t * GROUP + g, :, first_lane : first_lane + LANES],
                        (place - offset) % LANES,
                        1,
                    )
                    acc = jnp.where((lane >= place) & (lane < place + STRIP), moved, acc)
            packed[side, t] = acc

    pl.semaphore_wait(barrier, expected)

    def halo_copy(way):
        dx, dy = WAYS[way]
        if dy == 0:
            src = rc.at[:, pl.ds(HALO if dx < 0 else rows, HALO), :, pl.ds(0, cols)]
            dst = rc.at[:, pl.ds(HALO + rows if dx < 0 else 0, HALO), :, pl.ds(0, cols)]
        elif dx == 0:
            src = packed.at[0 if dy < 0 else 1]
            dst = side_in.at[0 if dy < 0 else 1]
        else:
            src = packed.at[0 if dy < 0 else 1, 0 if dx < 0 else tiles - 1]
            dst = corner_in.at[way - 4]
        return pltpu.make_async_remote_copy(
            src_ref=src, dst_ref=dst, send_sem=halo_send.at[way], recv_sem=halo_recv.at[way],
            device_id=(me_x + dx, me_y + dy), device_id_type=MESH,
        )

    order = (4, 5, 6, 7, 0, 1, 2, 3)
    for way in order:

        @pl.when(exists(*WAYS[way]))
        def _():
            halo_copy(way).start()

    for way in order:
        dx, dy = WAYS[way]
        absent = jnp.logical_not(exists(-dx, -dy))

        @pl.when(absent)
        def _():
            if dy == 0:
                low = HALO + rows if dx < 0 else 0
                rc[:, low : low + HALO, :, 0:cols] = jnp.zeros(
                    (2, HALO, levels, cols), jnp.float32
                )
            elif dx == 0:
                side_in[0 if dy < 0 else 1] = jnp.zeros((tiles, levels, LANES), jnp.float32)
            else:
                corner_in[way - 4] = jnp.zeros((levels, LANES), jnp.float32)

    for way in order:
        dx, dy = WAYS[way]

        @pl.when(exists(-dx, -dy))
        def _():
            halo_copy(way).wait_recv()

    for row in range(rows + 2 * HALO):
        if row < HALO:
            right, left, g = corner_in[2], corner_in[3], row + GROUP - HALO
        elif row < HALO + rows:
            t, g = divmod(row - HALO, GROUP)
            right, left = side_in[0, t], side_in[1, t]
        else:
            right, left, g = corner_in[0], corner_in[1], row - HALO - rows
        for a in range(2):
            place = (a * GROUP + g) * STRIP
            right_moved = pltpu.roll(right, (LANES - place) % LANES, 1)
            left_moved = pltpu.roll(left, (2 * LANES - STRIP - place) % LANES, 1)
            rc[a, row, :, cols:wide] = jnp.where(
                lane < STRIP, right_moved, jnp.where(lane >= LANES - STRIP, left_moved, 0.0)
            )

    field = rc.at[0]
    cond = rc.at[1]
    def around(v):
        return (
            pltpu.roll(v, 1, 2),
            pltpu.roll(v, wide - 1, 2),
            pltpu.roll(v, 1, 1),
            pltpu.roll(v, levels - 1, 1),
        )

    def coefficients(x, n):
        level = lax.broadcasted_iota(jnp.int32, (n, levels, wide), 1)
        c = cond[pl.ds(x, n)]
        west, east, below, above = around(c)
        below = jnp.where(level > 0, below, 0.0)
        above = jnp.where(level < levels - 1, above, 0.0)
        inside = c > 0.0
        faces = [
            jnp.where(inside, 0.5 * (c + other), 0.0)
            for other in (cond[pl.ds(x - 1, n)], cond[pl.ds(x + 1, n)], west, east, below, above)
        ]
        diag = ((faces[0] + faces[1]) + (faces[2] + faces[3])) + (faces[4] + faces[5])
        faces[4] = jnp.where(level > 0, faces[4], 0.0)
        faces[5] = jnp.where(level < levels - 1, faces[5], 0.0)
        return [diag] + faces

    def apply(ref, x, n, k):
        v = ref[pl.ds(x, n)]
        west, east, below, above = around(v)
        off = (
            (k[1] * ref[pl.ds(x - 1, n)] + k[2] * ref[pl.ds(x + 1, n)])
            + (k[3] * west + k[4] * east)
        ) + (k[5] * below + k[6] * above)
        return v, k[0] * v - off

    def kept(x, n):
        return [coef[i, pl.ds(x, n)] for i in range(7)]

    def sweep(low, body, carry=None):
        count, rest = divmod(rows + 2 * HALO - 2 * low, STEP)
        carry = lax.fori_loop(0, count, lambda i, s: body(low + i * STEP, STEP, s), carry)
        return body(low + count * STEP, rest, carry) if rest else carry

    def opening(ref, x, n, k):
        v, image = apply(ref, x, n, k)
        res_one = v - image * (1.0 / cheb_theta)
        res_f[pl.ds(x, n)] = res_one
        step_f[pl.ds(x, n)] = (
            (rho_second * rho_first / cheb_theta) * v + (2.0 * rho_second / cheb_delta) * res_one
        )

    def closing(source, out, x, n):
        step_one, image = apply(step_f, x, n, kept(x, n))
        res_two = res_f[pl.ds(x, n)] - image
        out[pl.ds(x, n)] = (
            (1.0 / cheb_theta) * source[pl.ds(x, n)]
            + (1.0 + rho_third * rho_second) * step_one
            + (2.0 * rho_third / cheb_delta) * res_two
        )

    def sweep_one(x, n, state):
        k = coefficients(x, n)
        for i in range(7):
            coef[i, pl.ds(x, n)] = k[i]
        opening(field, x, n, k)
        return state

    def sweep_two(x, n, state):
        closing(field, prec, x, n)
        return state

    def sweep_three(x, n, state):
        appl[pl.ds(x, n)] = apply(prec, x, n, kept(x, n))[1]
        return state

    def sweep_four(x, n, state):
        opening(appl, x, n, kept(x, n))
        return state

    def sweep_five(x, n, state):
        closing(appl, pre2, x, n)
        return state

    def folded(v):
        total = v[0]
        for i in range(1, v.shape[0]):
            total = total + v[i]
        parts = [total[:, i : i + LANES] for i in range(0, cols, LANES)]
        out = parts[0]
        for part in parts[1:]:
            out = out + part
        return out

    def sweep_six(x, n, state):
        m_all, i_all = apply(pre2, x, n, kept(x, n))
        img[pl.ds(x, n)] = i_all[:, :, 0:cols]
        m, q = m_all[:, :, 0:cols], i_all[:, :, 0:cols]
        r = field[pl.ds(x, n), :, 0:cols]
        p = prec[pl.ds(x, n), :, 0:cols]
        w = appl[pl.ds(x, n), :, 0:cols]
        products = (r * p, w * p, r * m, w * m, q * p, q * m)
        return tuple(s + folded(v) for s, v in zip(state, products))

    sweep(1, sweep_one)
    sweep(2, sweep_two)
    sweep(3, sweep_three)
    sweep(4, sweep_four)
    sweep(5, sweep_five)
    zero = jnp.zeros((levels, LANES), jnp.float32)
    sums = sweep(6, sweep_six, (zero,) * 6)

    line = lax.broadcasted_iota(jnp.int32, (8, LANES), 0)
    table = jnp.zeros((8, LANES), jnp.float32)
    for i, s in enumerate(sums):
        table = jnp.where(line == i, jnp.sum(s, axis=0, keepdims=True), table)
    msg[0] = table

    def turn(slot, ref):
        for t in range(tiles):
            turned[slot, :, t * GROUP : (t + 1) * GROUP, :] = jnp.transpose(
                ref[HALO + t * GROUP : HALO + (t + 1) * GROUP, :, 0:cols], (1, 0, 2)
            )

    copies = []
    for k in range(1, num_x):
        copies.append(pltpu.make_async_remote_copy(
            src_ref=msg.at[0], dst_ref=from_x.at[k - 1],
            send_sem=x_send.at[k - 1], recv_sem=x_recv.at[k - 1],
            device_id=(lax.rem(me_x + k, num_x), me_y), device_id_type=MESH,
        ))
    for copy in copies:
        copy.start()
    turn(0, prec)
    turn(1, appl)
    for copy in copies:
        copy.wait_recv()
    total = msg[0]
    for k in range(1, num_x):
        total = total + from_x[k - 1]
    msg[1] = total
    more = []
    for k in range(1, num_y):
        more.append(pltpu.make_async_remote_copy(
            src_ref=msg.at[1], dst_ref=from_y.at[k - 1],
            send_sem=y_send.at[k - 1], recv_sem=y_recv.at[k - 1],
            device_id=(me_x, lax.rem(me_y + k, num_y)), device_id_type=MESH,
        ))
    for copy in more:
        copy.start()
    turn(2, pre2)
    turn(3, img)
    for copy in more:
        copy.wait_recv()
    total = msg[1]
    for k in range(1, num_y):
        total = total + from_y[k - 1]

    def lanes_of(i):
        return total[i : i + 1, :]

    rp, wp, rm, wm, np_, nm = (lanes_of(i) for i in range(6))
    gamma_old = jnp.sum(rp, axis=1, keepdims=True)
    alpha_old = gamma_old / jnp.sum(wp, axis=1, keepdims=True)
    gamma = jnp.sum((rp - alpha_old * wp) - alpha_old * (rm - alpha_old * wm), axis=1, keepdims=True)
    delta = jnp.sum((wp - alpha_old * np_) - alpha_old * (wm - alpha_old * nm), axis=1, keepdims=True)
    beta = gamma / gamma_old
    alpha = gamma / (delta - beta * gamma / alpha_old)
    near = alpha_old + alpha * (1.0 + beta)
    far = alpha * alpha_old
    for z in range(levels):
        x_out[z] = near * turned[0, z] - far * turned[2, z]
        res_out[z] = (r_in[z] - near * turned[1, z]) + far * turned[3, z]

    for way in order:

        @pl.when(exists(*WAYS[way]))
        def _():
            halo_copy(way).wait_send()

    for copy in copies + more:
        copy.wait_send()


def solution(mesh):
    num_x, num_y = mesh.shape["gx"], mesh.shape["gy"]

    def per_device(right_side, conductivity):
        levels, rows, cols = right_side.shape
        high = rows + 2 * HALO
        wide = cols + LANES
        tiles = rows // GROUP

        def body(*refs):
            kernel(num_x, num_y, *refs)

        block = (levels, rows, cols)
        full = (high, levels, wide)
        out = jax.ShapeDtypeStruct(block, jnp.float32)
        vmem = lambda shape: pltpu.VMEM(shape, jnp.float32)
        dma = lambda n: pltpu.SemaphoreType.DMA((n,))
        return pl.pallas_call(
            body,
            out_shape=(out, out),
            in_specs=[pl.BlockSpec(memory_space=pltpu.HBM)] * 2,
            out_specs=(pl.BlockSpec(memory_space=pltpu.VMEM),) * 2,
            scratch_shapes=[
                vmem(block), vmem(block), vmem((2,) + full), vmem((7,) + full),
                vmem(full), vmem(full), vmem(full), vmem(full), vmem(full),
                vmem((high, levels, cols)),
                vmem((2, tiles, levels, LANES)), vmem((2, tiles, levels, LANES)),
                vmem((4, levels, LANES)), vmem((4,) + block),
                vmem((2, 8, LANES)), vmem((max(num_x - 1, 1), 8, LANES)),
                vmem((max(num_y - 1, 1), 8, LANES)),
                dma(2), dma(8), dma(8),
                dma(max(num_x - 1, 1)), dma(max(num_x - 1, 1)),
                dma(max(num_y - 1, 1)), dma(max(num_y - 1, 1)),
            ],
            compiler_params=pltpu.CompilerParams(
                collective_id=0, has_side_effects=True, vmem_limit_bytes=56000000
            ),
        )(right_side, conductivity)

    return jax.shard_map(
        per_device,
        mesh=mesh,
        in_specs=(P(None, "gx", "gy"), P(None, "gx", "gy")),
        out_specs=(P(None, "gx", "gy"), P(None, "gx", "gy")),
        check_vma=False,
    )
```

```python
import jax
import jax.numpy as jnp
from jax import lax
from jax.experimental import pallas as pl
from jax.experimental.pallas import tpu as pltpu
from jax.sharding import PartitionSpec as P

low_bound = 0.4
high_bound = 12.0
cheb_theta = 0.5 * (high_bound + low_bound)
cheb_delta = 0.5 * (high_bound - low_bound)
cheb_sigma = cheb_theta / cheb_delta
rho_first = 1.0 / cheb_sigma
rho_second = 1.0 / (2.0 * cheb_sigma - rho_first)
rho_third = 1.0 / (2.0 * cheb_sigma - rho_second)

HALO = 6
LANES = 128
STRIP = 8
GROUP = 8
STEP = 4
MESH = pl.DeviceIdType.MESH
WAYS = ((-1, 0), (1, 0), (0, -1), (0, 1), (-1, -1), (-1, 1), (1, -1), (1, 1))


def kernel(
    num_x, num_y, r_hbm, c_hbm, x_out, res_out,
    r_in, c_in, rc, coef, step_f, res_f, prec, appl, pre2, img,
    packed, side_in, corner_in, turned, msg, from_x, from_y,
    in_sem, halo_send, halo_recv, x_send, x_recv, y_send, y_recv,
):
    levels, rows, cols = r_in.shape
    wide = cols + LANES
    tiles = rows // GROUP
    me_x = lax.axis_index("gx")
    me_y = lax.axis_index("gy")

    def exists(dx, dy):
        ok = jnp.bool_(True)
        if dx < 0:
            ok = me_x > 0
        if dx > 0:
            ok = me_x < num_x - 1
        if dy < 0:
            ok_y = me_y > 0
            ok = ok_y if dx == 0 else jnp.logical_and(ok, ok_y)
        if dy > 0:
            ok_y = me_y < num_y - 1
            ok = ok_y if dx == 0 else jnp.logical_and(ok, ok_y)
        return ok

    loads = [
        pltpu.make_async_copy(r_hbm, r_in, in_sem.at[0]),
        pltpu.make_async_copy(c_hbm, c_in, in_sem.at[1]),
    ]
    for load in loads:
        load.start()

    barrier = pltpu.get_barrier_semaphore()
    expected = jnp.int32(num_x - 1 + num_y - 1)
    for dx, dy in WAYS[4:]:
        ok = exists(dx, dy)

        @pl.when(ok)
        def _():
            pl.semaphore_signal(
                barrier, inc=1, device_id=(me_x + dx, me_y + dy), device_id_type=MESH
            )

        expected = expected + ok.astype(jnp.int32)
    for k in range(1, num_x):
        pl.semaphore_signal(
            barrier, inc=1, device_id=(lax.rem(me_x + k, num_x), me_y), device_id_type=MESH
        )
    for k in range(1, num_y):
        pl.semaphore_signal(
            barrier, inc=1, device_id=(me_x, lax.rem(me_y + k, num_y)), device_id_type=MESH
        )

    lane = lax.broadcasted_iota(jnp.int32, (levels, LANES), 1)

    for load in loads:
        load.wait()
    for a, source in enumerate((r_in, c_in)):
        for t in range(tiles):
            rc[a, HALO + t * GROUP : HALO + (t + 1) * GROUP, :, 0:cols] = jnp.transpose(
                source[:, t * GROUP : (t + 1) * GROUP, :], (1, 0, 2)
            )
    for side in range(2):
        first_lane = 0 if side == 0 else cols - LANES
        offset = 0 if side == 0 else LANES - STRIP
        for t in range(tiles):
            acc = jnp.zeros((levels, LANES), jnp.float32)
            for a in range(2):
                for g in range(GROUP):
                    place = (a * GROUP + g) * STRIP
                    moved = pltpu.roll(
                        rc[a, HALO + t * GROUP + g, :, first_lane : first_lane + LANES],
                        (place - offset) % LANES,
                        1,
                    )
                    acc = jnp.where((lane >= place) & (lane < place + STRIP), moved, acc)
            packed[side, t] = acc

    pl.semaphore_wait(barrier, expected)

    def halo_copy(way):
        dx, dy = WAYS[way]
        if dy == 0:
            src = rc.at[:, pl.ds(HALO if dx < 0 else rows, HALO), :, pl.ds(0, cols)]
            dst = rc.at[:, pl.ds(HALO + rows if dx < 0 else 0, HALO), :, pl.ds(0, cols)]
        elif dx == 0:
            src = packed.at[0 if dy < 0 else 1]
            dst = side_in.at[0 if dy < 0 else 1]
        else:
            src = packed.at[0 if dy < 0 else 1, 0 if dx < 0 else tiles - 1]
            dst = corner_in.at[way - 4]
        return pltpu.make_async_remote_copy(
            src_ref=src, dst_ref=dst, send_sem=halo_send.at[way], recv_sem=halo_recv.at[way],
            device_id=(me_x + dx, me_y + dy), device_id_type=MESH,
        )

    order = (4, 5, 6, 7, 0, 1, 2, 3)
    for way in order:

        @pl.when(exists(*WAYS[way]))
        def _():
            halo_copy(way).start()

    for way in order:
        dx, dy = WAYS[way]
        absent = jnp.logical_not(exists(-dx, -dy))

        @pl.when(absent)
        def _():
            if dy == 0:
                low = HALO + rows if dx < 0 else 0
                rc[:, low : low + HALO, :, 0:cols] = jnp.zeros(
                    (2, HALO, levels, cols), jnp.float32
                )
            elif dx == 0:
                side_in[0 if dy < 0 else 1] = jnp.zeros((tiles, levels, LANES), jnp.float32)
            else:
                corner_in[way - 4] = jnp.zeros((levels, LANES), jnp.float32)

    for way in order:
        dx, dy = WAYS[way]

        @pl.when(exists(-dx, -dy))
        def _():
            halo_copy(way).wait_recv()

    for row in range(rows + 2 * HALO):
        if row < HALO:
            right, left, g = corner_in[2], corner_in[3], row + GROUP - HALO
        elif row < HALO + rows:
            t, g = divmod(row - HALO, GROUP)
            right, left = side_in[0, t], side_in[1, t]
        else:
            right, left, g = corner_in[0], corner_in[1], row - HALO - rows
        for a in range(2):
            place = (a * GROUP + g) * STRIP
            right_moved = pltpu.roll(right, (LANES - place) % LANES, 1)
            left_moved = pltpu.roll(left, (2 * LANES - STRIP - place) % LANES, 1)
            rc[a, row, :, cols:wide] = jnp.where(
                lane < STRIP, right_moved, jnp.where(lane >= LANES - STRIP, left_moved, 0.0)
            )

    field = rc.at[0]
    cond = rc.at[1]
    def around(v):
        return (
            pltpu.roll(v, 1, 2),
            pltpu.roll(v, wide - 1, 2),
            pltpu.roll(v, 1, 1),
            pltpu.roll(v, levels - 1, 1),
        )

    def coefficients(x, n):
        level = lax.broadcasted_iota(jnp.int32, (n, levels, wide), 1)
        c = cond[pl.ds(x, n)]
        west, east, below, above = around(c)
        below = jnp.where(level > 0, below, 0.0)
        above = jnp.where(level < levels - 1, above, 0.0)
        inside = c > 0.0
        faces = [
            jnp.where(inside, 0.5 * (c + other), 0.0)
            for other in (cond[pl.ds(x - 1, n)], cond[pl.ds(x + 1, n)], west, east, below, above)
        ]
        diag = ((faces[0] + faces[1]) + (faces[2] + faces[3])) + (faces[4] + faces[5])
        faces[4] = jnp.where(level > 0, faces[4], 0.0)
        faces[5] = jnp.where(level < levels - 1, faces[5], 0.0)
        return [diag] + faces

    def apply(ref, x, n, k):
        v = ref[pl.ds(x, n)]
        west, east, below, above = around(v)
        off = (
            (k[1] * ref[pl.ds(x - 1, n)] + k[2] * ref[pl.ds(x + 1, n)])
            + (k[3] * west + k[4] * east)
        ) + (k[5] * below + k[6] * above)
        return v, k[0] * v - off

    def kept(x, n):
        return [coef[i, pl.ds(x, n)] for i in range(7)]

    def sweep(low, body, carry=None):
        count, rest = divmod(rows + 2 * HALO - 2 * low, STEP)
        carry = lax.fori_loop(0, count, lambda i, s: body(low + i * STEP, STEP, s), carry)
        return body(low + count * STEP, rest, carry) if rest else carry

    def opening(ref, x, n, k):
        v, image = apply(ref, x, n, k)
        res_one = v - image * (1.0 / cheb_theta)
        res_f[pl.ds(x, n)] = res_one
        step_f[pl.ds(x, n)] = (
            (rho_second * rho_first / cheb_theta) * v + (2.0 * rho_second / cheb_delta) * res_one
        )

    def closing(source, out, x, n):
        step_one, image = apply(step_f, x, n, kept(x, n))
        res_two = res_f[pl.ds(x, n)] - image
        out[pl.ds(x, n)] = (
            (1.0 / cheb_theta) * source[pl.ds(x, n)]
            + (1.0 + rho_third * rho_second) * step_one
            + (2.0 * rho_third / cheb_delta) * res_two
        )

    def sweep_one(x, n, state):
        k = coefficients(x, n)
        for i in range(7):
            coef[i, pl.ds(x, n)] = k[i]
        opening(field, x, n, k)
        return state

    def sweep_two(x, n, state):
        closing(field, prec, x, n)
        return state

    def sweep_three(x, n, state):
        appl[pl.ds(x, n)] = apply(prec, x, n, kept(x, n))[1]
        return state

    def sweep_four(x, n, state):
        opening(appl, x, n, kept(x, n))
        return state

    def sweep_five(x, n, state):
        closing(appl, pre2, x, n)
        return state

    def folded(v):
        total = v[0]
        for i in range(1, v.shape[0]):
            total = total + v[i]
        parts = [total[:, i : i + LANES] for i in range(0, cols, LANES)]
        out = parts[0]
        for part in parts[1:]:
            out = out + part
        return out

    def sweep_six(x, n, state):
        m_all, i_all = apply(pre2, x, n, kept(x, n))
        img[pl.ds(x, n)] = i_all[:, :, 0:cols]
        m, q = m_all[:, :, 0:cols], i_all[:, :, 0:cols]
        r = field[pl.ds(x, n), :, 0:cols]
        p = prec[pl.ds(x, n), :, 0:cols]
        w = appl[pl.ds(x, n), :, 0:cols]
        products = (r * p, w * p, r * m, w * m, q * p, q * m)
        return tuple(s + folded(v) for s, v in zip(state, products))

    sweep(1, sweep_one)
    sweep(2, sweep_two)
    sweep(3, sweep_three)
    sweep(4, sweep_four)
    sweep(5, sweep_five)
    zero = jnp.zeros((levels, LANES), jnp.float32)
    sums = sweep(6, sweep_six, (zero,) * 6)

    line = lax.broadcasted_iota(jnp.int32, (8, LANES), 0)
    table = jnp.zeros((8, LANES), jnp.float32)
    for i, s in enumerate(sums):
        table = jnp.where(line == i, jnp.sum(s, axis=0, keepdims=True), table)
    msg[0] = table

    def turn(slot, ref):
        for t in range(tiles):
            turned[slot, :, t * GROUP : (t + 1) * GROUP, :] = jnp.transpose(
                ref[HALO + t * GROUP : HALO + (t + 1) * GROUP, :, 0:cols], (1, 0, 2)
            )

    copies = []
    for k in range(1, num_x):
        copies.append(pltpu.make_async_remote_copy(
            src_ref=msg.at[0], dst_ref=from_x.at[k - 1],
            send_sem=x_send.at[k - 1], recv_sem=x_recv.at[k - 1],
            device_id=(lax.rem(me_x + k, num_x), me_y), device_id_type=MESH,
        ))
    for copy in copies:
        copy.start()
    turn(0, prec)
    turn(1, appl)
    for copy in copies:
        copy.wait_recv()
    total = msg[0]
    for k in range(1, num_x):
        total = total + from_x[k - 1]
    msg[1] = total
    more = []
    for k in range(1, num_y):
        more.append(pltpu.make_async_remote_copy(
            src_ref=msg.at[1], dst_ref=from_y.at[k - 1],
            send_sem=y_send.at[k - 1], recv_sem=y_recv.at[k - 1],
            device_id=(me_x, lax.rem(me_y + k, num_y)), device_id_type=MESH,
        ))
    for copy in more:
        copy.start()
    turn(2, pre2)
    turn(3, img)
    for copy in more:
        copy.wait_recv()
    total = msg[1]
    for k in range(1, num_y):
        total = total + from_y[k - 1]

    def lanes_of(i):
        return total[i : i + 1, :]

    rp, wp, rm, wm, np_, nm = (lanes_of(i) for i in range(6))
    gamma_old = jnp.sum(rp, axis=1, keepdims=True)
    alpha_old = gamma_old / jnp.sum(wp, axis=1, keepdims=True)
    gamma = jnp.sum((rp - alpha_old * wp) - alpha_old * (rm - alpha_old * wm), axis=1, keepdims=True)
    delta = jnp.sum((wp - alpha_old * np_) - alpha_old * (wm - alpha_old * nm), axis=1, keepdims=True)
    beta = gamma / gamma_old
    alpha = gamma / (delta - beta * gamma / alpha_old)
    near = alpha_old + alpha * (1.0 + beta)
    far = alpha * alpha_old
    for z in range(levels):
        x_out[z] = near * turned[0, z] - far * turned[2, z]
        res_out[z] = (r_in[z] - near * turned[1, z]) + far * turned[3, z]

    for way in order:

        @pl.when(exists(*WAYS[way]))
        def _():
            halo_copy(way).wait_send()

    for copy in copies + more:
        copy.wait_send()


def solution(mesh):
    num_x, num_y = mesh.shape["gx"], mesh.shape["gy"]

    def per_device(right_side, conductivity):
        levels, rows, cols = right_side.shape
        high = rows + 2 * HALO
        wide = cols + LANES
        tiles = rows // GROUP

        def body(*refs):
            kernel(num_x, num_y, *refs)

        block = (levels, rows, cols)
        full = (high, levels, wide)
        out = jax.ShapeDtypeStruct(block, jnp.float32)
        vmem = lambda shape: pltpu.VMEM(shape, jnp.float32)
        dma = lambda n: pltpu.SemaphoreType.DMA((n,))
        return pl.pallas_call(
            body,
            out_shape=(out, out),
            in_specs=[pl.BlockSpec(memory_space=pltpu.HBM)] * 2,
            out_specs=(pl.BlockSpec(memory_space=pltpu.VMEM),) * 2,
            scratch_shapes=[
                vmem(block), vmem(block), vmem((2,) + full), vmem((7,) + full),
                vmem(full), vmem(full), vmem(full), vmem(full), vmem(full),
                vmem((high, levels, cols)),
                vmem((2, tiles, levels, LANES)), vmem((2, tiles, levels, LANES)),
                vmem((4, levels, LANES)), vmem((4,) + block),
                vmem((2, 8, LANES)), vmem((max(num_x - 1, 1), 8, LANES)),
                vmem((max(num_y - 1, 1), 8, LANES)),
                dma(2), dma(8), dma(8),
                dma(max(num_x - 1, 1)), dma(max(num_x - 1, 1)),
                dma(max(num_y - 1, 1)), dma(max(num_y - 1, 1)),
            ],
            compiler_params=pltpu.CompilerParams(
                collective_id=0, has_side_effects=True, vmem_limit_bytes=56000000
            ),
        )(right_side, conductivity)

    return jax.shard_map(
        per_device,
        mesh=mesh,
        in_specs=(P(None, "gx", "gy"), P(None, "gx", "gy")),
        out_specs=(P(None, "gx", "gy"), P(None, "gx", "gy")),
        check_vma=False,
    )
```

```python
import jax
import jax.numpy as jnp
from jax import lax
from jax.experimental import pallas as pl
from jax.experimental.pallas import tpu as pltpu
from jax.sharding import PartitionSpec as P

low_bound = 0.4
high_bound = 12.0
cheb_theta = 0.5 * (high_bound + low_bound)
cheb_delta = 0.5 * (high_bound - low_bound)
cheb_sigma = cheb_theta / cheb_delta
rho_first = 1.0 / cheb_sigma
rho_second = 1.0 / (2.0 * cheb_sigma - rho_first)
rho_third = 1.0 / (2.0 * cheb_sigma - rho_second)

HALO = 6
LANES = 128
STRIP = 8
GROUP = 8
STEP = 8
MESH = pl.DeviceIdType.MESH
WAYS = ((-1, 0), (1, 0), (0, -1), (0, 1), (-1, -1), (-1, 1), (1, -1), (1, 1))


def kernel(
    num_x, num_y, r_hbm, c_hbm, x_out, res_out,
    r_in, c_in, rc, coef, step_f, res_f, prec, appl, pre2, img,
    packed, side_in, corner_in, turned, msg, from_x, from_y,
    in_sem, halo_send, halo_recv, x_send, x_recv, y_send, y_recv,
):
    levels, rows, cols = r_in.shape
    wide = cols + LANES
    tiles = rows // GROUP
    me_x = lax.axis_index("gx")
    me_y = lax.axis_index("gy")

    def exists(dx, dy):
        ok = jnp.bool_(True)
        if dx < 0:
            ok = me_x > 0
        if dx > 0:
            ok = me_x < num_x - 1
        if dy < 0:
            ok_y = me_y > 0
            ok = ok_y if dx == 0 else jnp.logical_and(ok, ok_y)
        if dy > 0:
            ok_y = me_y < num_y - 1
            ok = ok_y if dx == 0 else jnp.logical_and(ok, ok_y)
        return ok

    loads = [
        pltpu.make_async_copy(r_hbm, r_in, in_sem.at[0]),
        pltpu.make_async_copy(c_hbm, c_in, in_sem.at[1]),
    ]
    for load in loads:
        load.start()

    barrier = pltpu.get_barrier_semaphore()
    expected = jnp.int32(num_x - 1 + num_y - 1)
    for dx, dy in WAYS[4:]:
        ok = exists(dx, dy)

        @pl.when(ok)
        def _():
            pl.semaphore_signal(
                barrier, inc=1, device_id=(me_x + dx, me_y + dy), device_id_type=MESH
            )

        expected = expected + ok.astype(jnp.int32)
    for k in range(1, num_x):
        pl.semaphore_signal(
            barrier, inc=1, device_id=(lax.rem(me_x + k, num_x), me_y), device_id_type=MESH
        )
    for k in range(1, num_y):
        pl.semaphore_signal(
            barrier, inc=1, device_id=(me_x, lax.rem(me_y + k, num_y)), device_id_type=MESH
        )

    lane = lax.broadcasted_iota(jnp.int32, (levels, LANES), 1)

    for load in loads:
        load.wait()
    for a, source in enumerate((r_in, c_in)):
        for t in range(tiles):
            rc[a, HALO + t * GROUP : HALO + (t + 1) * GROUP, :, 0:cols] = jnp.transpose(
                source[:, t * GROUP : (t + 1) * GROUP, :], (1, 0, 2)
            )
    for side in range(2):
        first_lane = 0 if side == 0 else cols - LANES
        offset = 0 if side == 0 else LANES - STRIP
        for t in range(tiles):
            acc = jnp.zeros((levels, LANES), jnp.float32)
            for a in range(2):
                for g in range(GROUP):
                    place = (a * GROUP + g) * STRIP
                    moved = pltpu.roll(
                        rc[a, HALO + t * GROUP + g, :, first_lane : first_lane + LANES],
                        (place - offset) % LANES,
                        1,
                    )
                    acc = jnp.where((lane >= place) & (lane < place + STRIP), moved, acc)
            packed[side, t] = acc

    pl.semaphore_wait(barrier, expected)

    def halo_copy(way):
        dx, dy = WAYS[way]
        if dy == 0:
            src = rc.at[:, pl.ds(HALO if dx < 0 else rows, HALO), :, pl.ds(0, cols)]
            dst = rc.at[:, pl.ds(HALO + rows if dx < 0 else 0, HALO), :, pl.ds(0, cols)]
        elif dx == 0:
            src = packed.at[0 if dy < 0 else 1]
            dst = side_in.at[0 if dy < 0 else 1]
        else:
            src = packed.at[0 if dy < 0 else 1, 0 if dx < 0 else tiles - 1]
            dst = corner_in.at[way - 4]
        return pltpu.make_async_remote_copy(
            src_ref=src, dst_ref=dst, send_sem=halo_send.at[way], recv_sem=halo_recv.at[way],
            device_id=(me_x + dx, me_y + dy), device_id_type=MESH,
        )

    order = (4, 5, 6, 7, 0, 1, 2, 3)
    for way in order:

        @pl.when(exists(*WAYS[way]))
        def _():
            halo_copy(way).start()

    for way in order:
        dx, dy = WAYS[way]
        absent = jnp.logical_not(exists(-dx, -dy))

        @pl.when(absent)
        def _():
            if dy == 0:
                low = HALO + rows if dx < 0 else 0
                rc[:, low : low + HALO, :, 0:cols] = jnp.zeros(
                    (2, HALO, levels, cols), jnp.float32
                )
            elif dx == 0:
                side_in[0 if dy < 0 else 1] = jnp.zeros((tiles, levels, LANES), jnp.float32)
            else:
                corner_in[way - 4] = jnp.zeros((levels, LANES), jnp.float32)

    for way in order:
        dx, dy = WAYS[way]

        @pl.when(exists(-dx, -dy))
        def _():
            halo_copy(way).wait_recv()

    for row in range(rows + 2 * HALO):
        if row < HALO:
            right, left, g = corner_in[2], corner_in[3], row + GROUP - HALO
        elif row < HALO + rows:
            t, g = divmod(row - HALO, GROUP)
            right, left = side_in[0, t], side_in[1, t]
        else:
            right, left, g = corner_in[0], corner_in[1], row - HALO - rows
        for a in range(2):
            place = (a * GROUP + g) * STRIP
            right_moved = pltpu.roll(right, (LANES - place) % LANES, 1)
            left_moved = pltpu.roll(left, (2 * LANES - STRIP - place) % LANES, 1)
            rc[a, row, :, cols:wide] = jnp.where(
                lane < STRIP, right_moved, jnp.where(lane >= LANES - STRIP, left_moved, 0.0)
            )

    field = rc.at[0]
    cond = rc.at[1]
    def around(v):
        return (
            pltpu.roll(v, 1, 2),
            pltpu.roll(v, wide - 1, 2),
            pltpu.roll(v, 1, 1),
            pltpu.roll(v, levels - 1, 1),
        )

    def coefficients(x, n):
        level = lax.broadcasted_iota(jnp.int32, (n, levels, wide), 1)
        c = cond[pl.ds(x, n)]
        west, east, below, above = around(c)
        below = jnp.where(level > 0, below, 0.0)
        above = jnp.where(level < levels - 1, above, 0.0)
        inside = c > 0.0
        faces = [
            jnp.where(inside, 0.5 * (c + other), 0.0)
            for other in (cond[pl.ds(x - 1, n)], cond[pl.ds(x + 1, n)], west, east, below, above)
        ]
        diag = ((faces[0] + faces[1]) + (faces[2] + faces[3])) + (faces[4] + faces[5])
        faces[4] = jnp.where(level > 0, faces[4], 0.0)
        faces[5] = jnp.where(level < levels - 1, faces[5], 0.0)
        return [diag] + faces

    def apply(ref, x, n, k):
        v = ref[pl.ds(x, n)]
        west, east, below, above = around(v)
        off = (
            (k[1] * ref[pl.ds(x - 1, n)] + k[2] * ref[pl.ds(x + 1, n)])
            + (k[3] * west + k[4] * east)
        ) + (k[5] * below + k[6] * above)
        return v, k[0] * v - off

    def kept(x, n):
        return [coef[i, pl.ds(x, n)] for i in range(7)]

    def sweep(low, body, carry=None):
        count, rest = divmod(rows + 2 * HALO - 2 * low, STEP)
        carry = lax.fori_loop(0, count, lambda i, s: body(low + i * STEP, STEP, s), carry)
        return body(low + count * STEP, rest, carry) if rest else carry

    def opening(ref, x, n, k):
        v, image = apply(ref, x, n, k)
        res_one = v - image * (1.0 / cheb_theta)
        res_f[pl.ds(x, n)] = res_one
        step_f[pl.ds(x, n)] = (
            (rho_second * rho_first / cheb_theta) * v + (2.0 * rho_second / cheb_delta) * res_one
        )

    def closing(source, out, x, n):
        step_one, image = apply(step_f, x, n, kept(x, n))
        res_two = res_f[pl.ds(x, n)] - image
        out[pl.ds(x, n)] = (
            (1.0 / cheb_theta) * source[pl.ds(x, n)]
            + (1.0 + rho_third * rho_second) * step_one
            + (2.0 * rho_third / cheb_delta) * res_two
        )

    def sweep_one(x, n, state):
        k = coefficients(x, n)
        for i in range(7):
            coef[i, pl.ds(x, n)] = k[i]
        opening(field, x, n, k)
        return state

    def sweep_two(x, n, state):
        closing(field, prec, x, n)
        return state

    def sweep_three(x, n, state):
        appl[pl.ds(x, n)] = apply(prec, x, n, kept(x, n))[1]
        return state

    def sweep_four(x, n, state):
        opening(appl, x, n, kept(x, n))
        return state

    def sweep_five(x, n, state):
        closing(appl, pre2, x, n)
        return state

    def folded(v):
        total = v[0]
        for i in range(1, v.shape[0]):
            total = total + v[i]
        parts = [total[:, i : i + LANES] for i in range(0, cols, LANES)]
        out = parts[0]
        for part in parts[1:]:
            out = out + part
        return out

    def sweep_six(x, n, state):
        m_all, i_all = apply(pre2, x, n, kept(x, n))
        img[pl.ds(x, n)] = i_all[:, :, 0:cols]
        m, q = m_all[:, :, 0:cols], i_all[:, :, 0:cols]
        r = field[pl.ds(x, n), :, 0:cols]
        p = prec[pl.ds(x, n), :, 0:cols]
        w = appl[pl.ds(x, n), :, 0:cols]
        products = (r * p, w * p, r * m, w * m, q * p, q * m)
        return tuple(s + folded(v) for s, v in zip(state, products))

    sweep(1, sweep_one)
    sweep(2, sweep_two)
    sweep(3, sweep_three)
    sweep(4, sweep_four)
    sweep(5, sweep_five)
    zero = jnp.zeros((levels, LANES), jnp.float32)
    sums = sweep(6, sweep_six, (zero,) * 6)

    line = lax.broadcasted_iota(jnp.int32, (8, LANES), 0)
    table = jnp.zeros((8, LANES), jnp.float32)
    for i, s in enumerate(sums):
        table = jnp.where(line == i, jnp.sum(s, axis=0, keepdims=True), table)
    msg[0] = table

    def turn(slot, ref):
        for t in range(tiles):
            turned[slot, :, t * GROUP : (t + 1) * GROUP, :] = jnp.transpose(
                ref[HALO + t * GROUP : HALO + (t + 1) * GROUP, :, 0:cols], (1, 0, 2)
            )

    copies = []
    for k in range(1, num_x):
        copies.append(pltpu.make_async_remote_copy(
            src_ref=msg.at[0], dst_ref=from_x.at[k - 1],
            send_sem=x_send.at[k - 1], recv_sem=x_recv.at[k - 1],
            device_id=(lax.rem(me_x + k, num_x), me_y), device_id_type=MESH,
        ))
    for copy in copies:
        copy.start()
    turn(0, prec)
    turn(1, appl)
    for copy in copies:
        copy.wait_recv()
    total = msg[0]
    for k in range(1, num_x):
        total = total + from_x[k - 1]
    msg[1] = total
    more = []
    for k in range(1, num_y):
        more.append(pltpu.make_async_remote_copy(
            src_ref=msg.at[1], dst_ref=from_y.at[k - 1],
            send_sem=y_send.at[k - 1], recv_sem=y_recv.at[k - 1],
            device_id=(me_x, lax.rem(me_y + k, num_y)), device_id_type=MESH,
        ))
    for copy in more:
        copy.start()
    turn(2, pre2)
    turn(3, img)
    for copy in more:
        copy.wait_recv()
    total = msg[1]
    for k in range(1, num_y):
        total = total + from_y[k - 1]

    def lanes_of(i):
        return total[i : i + 1, :]

    rp, wp, rm, wm, np_, nm = (lanes_of(i) for i in range(6))
    gamma_old = jnp.sum(rp, axis=1, keepdims=True)
    alpha_old = gamma_old / jnp.sum(wp, axis=1, keepdims=True)
    gamma = jnp.sum((rp - alpha_old * wp) - alpha_old * (rm - alpha_old * wm), axis=1, keepdims=True)
    delta = jnp.sum((wp - alpha_old * np_) - alpha_old * (wm - alpha_old * nm), axis=1, keepdims=True)
    beta = gamma / gamma_old
    alpha = gamma / (delta - beta * gamma / alpha_old)
    near = alpha_old + alpha * (1.0 + beta)
    far = alpha * alpha_old
    for z in range(levels):
        x_out[z] = near * turned[0, z] - far * turned[2, z]
        res_out[z] = (r_in[z] - near * turned[1, z]) + far * turned[3, z]

    for way in order:

        @pl.when(exists(*WAYS[way]))
        def _():
            halo_copy(way).wait_send()

    for copy in copies + more:
        copy.wait_send()


def solution(mesh):
    num_x, num_y = mesh.shape["gx"], mesh.shape["gy"]

    def per_device(right_side, conductivity):
        levels, rows, cols = right_side.shape
        high = rows + 2 * HALO
        wide = cols + LANES
        tiles = rows // GROUP

        def body(*refs):
            kernel(num_x, num_y, *refs)

        block = (levels, rows, cols)
        full = (high, levels, wide)
        out = jax.ShapeDtypeStruct(block, jnp.float32)
        vmem = lambda shape: pltpu.VMEM(shape, jnp.float32)
        dma = lambda n: pltpu.SemaphoreType.DMA((n,))
        return pl.pallas_call(
            body,
            out_shape=(out, out),
            in_specs=[pl.BlockSpec(memory_space=pltpu.HBM)] * 2,
            out_specs=(pl.BlockSpec(memory_space=pltpu.VMEM),) * 2,
            scratch_shapes=[
                vmem(block), vmem(block), vmem((2,) + full), vmem((7,) + full),
                vmem(full), vmem(full), vmem(full), vmem(full), vmem(full),
                vmem((high, levels, cols)),
                vmem((2, tiles, levels, LANES)), vmem((2, tiles, levels, LANES)),
                vmem((4, levels, LANES)), vmem((4,) + block),
                vmem((2, 8, LANES)), vmem((max(num_x - 1, 1), 8, LANES)),
                vmem((max(num_y - 1, 1), 8, LANES)),
                dma(2), dma(8), dma(8),
                dma(max(num_x - 1, 1)), dma(max(num_x - 1, 1)),
                dma(max(num_y - 1, 1)), dma(max(num_y - 1, 1)),
            ],
            compiler_params=pltpu.CompilerParams(
                collective_id=0, has_side_effects=True, vmem_limit_bytes=56000000
            ),
        )(right_side, conductivity)

    return jax.shard_map(
        per_device,
        mesh=mesh,
        in_specs=(P(None, "gx", "gy"), P(None, "gx", "gy")),
        out_specs=(P(None, "gx", "gy"), P(None, "gx", "gy")),
        check_vma=False,
    )
```
